512 devices in a mesh: seq: 64 (over y, x, core), tensor: 8 (over z).
Axes of the slice: x: 4, y: 8, z: 8, core: 2. Of those that a mesh axis runs over, the one named last changes fastest.
Arguments:
- query_rows: bfloat16 [8192, 4096], P('seq', 'tensor'), may hold values from -6 to 6
- key_rows: bfloat16 [8192, 4096], P('seq', 'tensor'), may hold values from -6 to 6
- value_rows: bfloat16 [8192, 4096], P('seq', 'tensor'), may hold values from -18 to 18
- cluster_id: int32 [32, 8192], P('tensor', 'seq'), may hold values from 0 to 511, as said below
- slot_index: int32 [32, 8192], P('tensor', 'seq'), may hold values from 0 to 31, as said below
- out_weight: bfloat16 [4096, 2048], P('tensor', 'seq'), may hold values from -0.09375 to 0.09375
- grad_out: bfloat16 [8192, 2048], P(('seq', 'tensor')), may hold values from -6 to 6
Outputs:
- mixed: bfloat16 [8192, 2048], P(('seq', 'tensor'))
- grad_query: bfloat16 [8192, 4096], P('seq', 'tensor')
- grad_key: bfloat16 [8192, 4096], P('seq', 'tensor')
- grad_value: bfloat16 [8192, 4096], P('seq', 'tensor')
The draws below stay inside these ranges and needn't reach their ends.
Inputs may be any that keep to these rules, and one draw needn't show every extreme that they name: `cluster_id`: cluster c of a head belongs to the index c // 8 of seq. Each cluster of a head holds at most 32 tokens and in every head some cluster holds exactly 32. The tokens of one index of seq go, for one head, to at most 4 slots among the clusters of one owner, and every index of seq reaches 4 for some owner in every head. `slot_index`: within one head and cluster the slots of its tokens are distinct.
All inputs are finite; a program needn't handle non-finite values.
Results may differ from the reference program's by a relative error of at most 0.025.
Values may be sent and summed in bfloat16 or wider, within the bound.
A program may use at most 64 MiB of HBM per device.

```python
import math
import jax
import jax.numpy as jnp
from jax import lax

H = 32
DH = 128
D_OUT = 2048
CLU_DEV = 8
TOK_DEV = 128
CAP = 32
CLUSTERS = 512
TOKENS = 8192
N_SEQ = 64


def route_table(key):
    owners = N_SEQ
    pair_total = 2 * (TOK_DEV // N_SEQ)
    room = CLU_DEV * CAP

    def one_sender(sender_key):
        first_key, second_key, third_key = jax.random.split(sender_key, 3)
        order = jax.random.permutation(first_key, owners)
        shares = jax.random.randint(second_key, (owners // 2,), 0, pair_total + 1)
        shares = shares.at[0].set(pair_total)
        counts = jnp.zeros((owners,), jnp.int32).at[order[0::2]].set(shares).at[order[1::2]].set(pair_total - shares)
        bounds = jnp.cumsum(counts)
        sorted_owner = jnp.searchsorted(bounds, jnp.arange(TOK_DEV, dtype=jnp.int32), side='right').astype(jnp.int32)
        shuffle = jax.random.permutation(third_key, TOK_DEV)
        owner = jnp.zeros((TOK_DEV,), jnp.int32).at[shuffle].set(sorted_owner)
        return (owner, counts)

    def one_head(head_key):
        sender_keys = jax.random.split(jax.random.fold_in(head_key, 0), owners)
        owner, counts = jax.vmap(one_sender)(sender_keys)
        onehot = (owner[:, :, None] == jnp.arange(owners, dtype=jnp.int32)[None, None, :]).astype(jnp.int32)
        rank = jnp.sum((jnp.cumsum(onehot, axis=1) - onehot) * onehot, axis=2)
        offsets = jnp.cumsum(counts, axis=0) - counts
        arrival = rank + jnp.take_along_axis(offsets, owner, axis=1)
        favored = jax.random.randint(jax.random.fold_in(head_key, 1), (owners,), 0, CLU_DEV)
        ranks = jax.vmap(lambda owner_key: jax.random.permutation(owner_key, room))(jax.random.split(jax.random.fold_in(head_key, 2), owners))
        cell_of = jnp.arange(room, dtype=jnp.int32) // CAP
        ranks = ranks + jnp.where(cell_of[None, :] == favored[:, None], 0, room)
        layout = jnp.argsort(ranks, axis=1, stable=True).astype(jnp.int32)
        position = layout[owner, arrival]
        cluster = owner * CLU_DEV + position // CAP
        return (cluster.reshape(-1).astype(jnp.int32), (position % CAP).reshape(-1).astype(jnp.int32))
    return lax.map(one_head, jax.random.split(key, H))


def draw_cluster_id(key, part):
    return route_table(jax.random.fold_in(key, 7))[0]


def draw_slot_index(key, part):
    return route_table(jax.random.fold_in(key, 7))[1]


def attention_rows(key, for_keys):
    base = jnp.clip(jax.random.normal(jax.random.fold_in(key, 11 + for_keys), (TOKENS, H * DH), jnp.float32), -6.0, 6.0)
    return base


def draw_query_rows(key, part):
    return attention_rows(key, 0).astype(jnp.bfloat16)


def draw_key_rows(key, part):
    return attention_rows(key, 1).astype(jnp.bfloat16)


def shard_levels(key, dims, cuts, least, high):
    loudness, own = 1.0, jax.random.fold_in(key, 6)
    for dim, shards_of in cuts:
        steps = jnp.exp(jax.random.uniform(jax.random.fold_in(own, dim), (shards_of,), jnp.float32, least / len(cuts), high / len(cuts)))
        loudness = loudness * jnp.repeat(steps, dims[dim] // shards_of).reshape([-1 if axis == dim else 1 for axis in range(len(dims))])
    return loudness


def normal_values(key, shape, spread, most, cuts=(), kind=jnp.bfloat16):
    values = jax.random.normal(key, shape, jnp.float32) * spread
    if len(cuts) > 0:
        values = shard_levels(key, shape, cuts, -0.22, 0.18) * values
    return jnp.clip(values, min=-most, max=most).astype(kind)


def setup_inputs(seed: int = 0) -> dict:
    arg_keys = jax.random.split(jax.random.key(seed), 8)
    query_rows = draw_query_rows(jax.random.fold_in(arg_keys[7], 71), 0)
    key_rows = draw_key_rows(jax.random.fold_in(arg_keys[7], 71), 0)
    value_rows = normal_values(arg_keys[2], (TOKENS, H * DH), 3.0, 18.0, ((0, 64), (1, 8)))
    cluster_id = draw_cluster_id(jax.random.fold_in(arg_keys[7], 71), 0)
    slot_index = draw_slot_index(jax.random.fold_in(arg_keys[7], 71), 0)
    out_weight = normal_values(arg_keys[5], (H * DH, D_OUT), (H * DH) ** -0.5, 0.09375, ((0, 8), (1, 64)))
    grad_out = normal_values(arg_keys[6], (TOKENS, D_OUT), 1.0, 6.0, ((0, 512),))
    return dict(query_rows=query_rows, key_rows=key_rows, value_rows=value_rows, cluster_id=cluster_id, slot_index=slot_index, out_weight=out_weight, grad_out=grad_out)


def reference(query_rows, key_rows, value_rows, cluster_id, slot_index, out_weight, grad_out):
    score_scale = 1.0 / math.sqrt(DH)
    masked_score = -1e+30
    room = CLUSTERS * CAP
    grad_attended = jnp.dot(grad_out, out_weight.T, preferred_element_type=jnp.float32).astype(jnp.bfloat16)

    def one_head(head):
        start = head * DH
        query_head = lax.dynamic_slice_in_dim(query_rows, start, DH, 1)
        key_head = lax.dynamic_slice_in_dim(key_rows, start, DH, 1)
        value_head = lax.dynamic_slice_in_dim(value_rows, start, DH, 1)
        grad_head = lax.dynamic_slice_in_dim(grad_attended, start, DH, 1)
        position = (cluster_id[head] * CAP + slot_index[head]).astype(jnp.int32)

        def to_cells(rows):
            return jnp.zeros((room, DH), rows.dtype).at[position].set(rows).reshape(CLUSTERS, CAP, DH)
        live = jnp.zeros((room,), jnp.float32).at[position].set(1.0).reshape(CLUSTERS, CAP)
        query_cells = to_cells(query_head).astype(jnp.float32)
        key_cells = to_cells(key_head).astype(jnp.float32)
        value_cells = to_cells(value_head).astype(jnp.float32)
        grad_cells = to_cells(grad_head).astype(jnp.float32)
        scores = jnp.einsum('cqd,ckd->cqk', query_cells, key_cells) * score_scale
        scores = jnp.where(live[:, None, :] > 0.5, scores, masked_score)
        top = lax.optimization_barrier(jnp.max(scores, axis=-1, keepdims=True))
        weights = jnp.exp(scores - top)
        probs = weights / lax.optimization_barrier(jnp.sum(weights, axis=-1, keepdims=True))
        probs_low = probs.astype(jnp.bfloat16).astype(jnp.float32)
        attended = jnp.einsum('cqk,ckd->cqd', probs_low, value_cells).astype(jnp.bfloat16)
        delta = jnp.einsum('cqd,cqd->cq', grad_cells, attended.astype(jnp.float32))
        grad_value = jnp.einsum('cqk,cqd->ckd', probs_low, grad_cells).astype(jnp.bfloat16)
        grad_probs = jnp.einsum('cqd,ckd->cqk', grad_cells, value_cells)
        grad_scores = (probs * (grad_probs - delta[..., None])).astype(jnp.bfloat16).astype(jnp.float32)
        grad_query = (jnp.einsum('cqk,ckd->cqd', grad_scores, key_cells) * score_scale).astype(jnp.bfloat16)
        grad_key = (jnp.einsum('cqk,cqd->ckd', grad_scores, query_cells) * score_scale).astype(jnp.bfloat16)

        def back(cells):
            return cells.reshape(room, DH)[position]
        return (back(attended), back(grad_query), back(grad_key), back(grad_value))
    stacks = lax.map(one_head, jnp.arange(H, dtype=jnp.int32))

    def merge_heads(stack):
        return jnp.transpose(stack, (1, 0, 2)).reshape(TOKENS, H * DH)
    attended_all = merge_heads(stacks[0])
    mixed = jnp.dot(attended_all, out_weight, preferred_element_type=jnp.float32).astype(jnp.bfloat16)
    return (mixed, merge_heads(stacks[1]), merge_heads(stacks[2]), merge_heads(stacks[3]))
```

```python
import functools
import math

import jax
import jax.numpy as jnp
from jax import lax
from jax.experimental import pallas as pl
from jax.experimental.pallas import tpu as pltpu
from jax.sharding import PartitionSpec as P

CLU_DEV = 8
SLOTS = 4
MESH = pl.DeviceIdType.MESH
F32 = jnp.float32
BF16 = jnp.bfloat16
NN = (((1,), (0,)), ((), ()))
NT = (((1,), (1,)), ((), ()))
TN = (((0,), (0,)), ((), ()))


def dot(a, b, dims=NN):
    return lax.dot_general(a, b, dims, preferred_element_type=F32)


def iota(shape, dim):
    return lax.broadcasted_iota(jnp.int32, shape, dim)


def kernel(
    dims,
    q_ref,
    k_ref,
    v_ref,
    cid_ref,
    w_ref,
    go_ref,
    mixed_ref,
    dq_ref,
    dk_ref,
    dv_ref,
    xcat,
    pack,
    unpack,
    msnd,
    mrcv,
    snd1,
    rcv1,
    sndg,
    rcvg,
    snda,
    rcva,
    sndb,
    rcvb,
    wt,
    gout,
    rsnd,
    rrcv,
    cells,
    probs,
    outs,
    ssem,
    rsem,
):
    ny, nx, nt, heads, tok, dh = dims
    ns = ny * nx * 2
    blk = heads * SLOTS
    peers = min(16, ns)
    chunks = ns // peers
    rows = peers * blk
    part = peers * SLOTS
    recv_rows = ns * SLOTS
    scale = 1.0 / math.sqrt(dh)
    me = lax.axis_index("seq")
    mt = lax.axis_index("tensor")
    my = lax.div(me, 2 * nx)
    mx = lax.rem(lax.div(me, 2), nx)
    mc = lax.rem(me, 2)

    barrier = pltpu.get_barrier_semaphore()

    def greet_seq(j, carry):
        pl.semaphore_signal(
            barrier, inc=1, device_id={"seq": lax.rem(me + j, ns)}, device_id_type=MESH
        )
        return carry

    lax.fori_loop(1, ns, greet_seq, 0)

    def greet_tensor(j, carry):
        pl.semaphore_signal(
            barrier, inc=1, device_id={"tensor": lax.rem(mt + j, nt)}, device_id_type=MESH
        )
        return carry

    lax.fori_loop(1, nt, greet_tensor, 0)

    def remote(src, dst, index, target):
        return pltpu.make_async_remote_copy(
            src_ref=src,
            dst_ref=dst,
            send_sem=ssem.at[index],
            recv_sem=rsem.at[index],
            device_id=target,
            device_id_type=MESH,
        )

    def wait_recv(ref, index):
        pltpu.make_async_copy(ref, ref, rsem.at[index]).wait()

    def wait_send(ref, index):
        pltpu.make_async_copy(ref, ref, ssem.at[index]).wait()

    def exchange(src, dst, index):
        def step(j, carry):
            ahead = lax.rem(me + j, ns)
            behind = lax.rem(me + ns - j, ns)
            remote(src.at[ahead], dst.at[me], index, {"seq": ahead}).start()
            remote(src.at[behind], dst.at[me], index, {"seq": behind}).start()
            return carry

        lax.fori_loop(1, ns // 2, step, 0)
        far = lax.rem(me + ns // 2, ns)
        remote(src.at[far], dst.at[me], index, {"seq": far}).start()

    wt[my, mx, mc] = dot(
        (iota((32, 32), 0) == iota((32, 32), 1)).astype(BF16), w_ref[...], NT
    ).astype(BF16)
    gout[mt] = go_ref[...]

    upper = (iota((tok, tok), 0) < iota((tok, tok), 1)).astype(BF16)
    diag = iota((tok, tok), 0) == iota((tok, tok), 1)
    table = jnp.zeros((ns, 128), F32)
    for h in range(heads):
        cid = cid_ref[h : h + 1, :]
        owner = lax.shift_right_logical(cid, 3)
        member = iota((ns, tok), 0) == owner
        onehot = member.astype(F32)
        earlier = dot(onehot.astype(BF16), upper)
        rank = jnp.sum(onehot * earlier, axis=0, keepdims=True).astype(jnp.int32)
        dest = owner * blk + h * SLOTS + rank
        for c in range(chunks):
            pack[c, :, h * tok : (h + 1) * tok] = (
                iota((rows, tok), 0) + c * rows == dest
            ).astype(BF16)
        column = jnp.sum(jnp.where(diag, dest, 0).astype(F32), axis=1, keepdims=True).astype(
            jnp.int32
        )
        unpack[h] = (iota((tok, ns * blk), 1) == column).astype(BF16)
        value = jnp.where(member, (cid & (CLU_DEV - 1)) + 1, 0).astype(F32).astype(BF16)
        lane = (iota((128, tok), 0) == rank + h * SLOTS).astype(BF16)
        table = table + dot(value, lane, NT)
        for t, ref in enumerate((q_ref, k_ref, v_ref)):
            xcat[h * tok : (h + 1) * tok, t * dh : (t + 1) * dh] = ref[:, h * dh : (h + 1) * dh]
    msnd[...] = table.reshape(ns, 1, 128)

    def pack_rows(c, carry):
        packed = dot(pack[c], xcat[...]).astype(BF16)
        for t in range(3):
            snd1[pl.ds(c * peers, peers), t] = packed[:, t * dh : (t + 1) * dh].reshape(
                peers, blk, dh
            )
        return carry

    lax.fori_loop(0, chunks, pack_rows, 0)

    pl.semaphore_wait(barrier, ns - 1 + nt - 1)

    def weight_y(j, carry):
        target = (lax.rem(my + j, ny) * nx + mx) * 2 + mc
        remote(wt.at[my, mx, mc], wt.at[my, mx, mc], 0, {"seq": target}).start()
        return carry

    lax.fori_loop(1, ny, weight_y, 0)

    def cotangent(j, carry):
        remote(gout.at[mt], gout.at[mt], 3, {"tensor": lax.rem(mt + j, nt)}).start()
        return carry

    lax.fori_loop(1, nt, cotangent, 0)

    exchange(msnd, mrcv, 4)
    exchange(snd1, rcv1, 5)
    mrcv[me] = msnd[me]
    rcv1[me] = snd1[me]

    wait_recv(wt.at[pl.ds(0, ny - 1), 0, 0], 0)

    def weight_x(j, carry):
        target = (my * nx + lax.rem(mx + j, nx)) * 2 + mc
        remote(wt.at[:, mx, mc], wt.at[:, mx, mc], 1, {"seq": target}).start()
        return carry

    lax.fori_loop(1, nx, weight_x, 0)
    wait_recv(wt.at[:, pl.ds(0, nx - 1), 0], 1)
    other = me + 1 - 2 * mc
    remote(wt.at[:, :, mc], wt.at[:, :, mc], 2, {"seq": other}).start()
    wait_recv(wt.at[:, :, 0], 2)
    wait_recv(gout.at[pl.ds(0, nt - 1)], 3)

    columns = nx * 2 * 32
    grad = jnp.zeros((tok, heads * dh), F32)
    for y in range(ny):
        grad = grad + dot(
            gout[:, :, y * columns : (y + 1) * columns].reshape(tok, columns),
            wt[y].reshape(columns, heads * dh),
        )
    grad = grad.astype(BF16)
    for h in range(heads):
        xcat[h * tok : (h + 1) * tok, :dh] = grad[:, h * dh : (h + 1) * dh]

    def pack_grad(c, carry):
        sndg[pl.ds(c * peers, peers)] = (
            dot(pack[c], xcat[:, :dh]).astype(BF16).reshape(peers, blk, dh)
        )
        return carry

    lax.fori_loop(0, chunks, pack_grad, 0)
    exchange(sndg, rcvg, 6)
    rcvg[me] = sndg[me]

    def source(index):
        h = lax.div(index, part)
        rest = index - h * part
        p = lax.div(rest, SLOTS)
        return p * blk + h * SLOTS + (rest - p * SLOTS)

    to_heads = (source(iota((rows, 1), 0)) == iota((rows, rows), 1)).astype(BF16)
    to_peers = (source(iota((1, rows), 1)) == iota((rows, rows), 0)).astype(BF16)

    wait_recv(mrcv.at[pl.ds(0, ns - 1)], 4)
    wait_recv(rcv1.at[pl.ds(0, ns - 1)], 5)

    lanes = iota((rows, 128), 1)
    own_lane = lanes == (iota((rows, 128), 0) & (blk - 1))

    def by_head(c, index, values):
        moved = dot(to_heads, values).astype(BF16)
        for h in range(heads):
            cells[index, h, c] = moved[h * part : (h + 1) * part]

    def split_heads(c, carry):
        spread = jnp.broadcast_to(
            mrcv[pl.ds(c * peers, peers)], (peers, blk, 128)
        ).reshape(rows, 128)
        mark = jnp.sum(jnp.where(own_lane, spread, 0.0), axis=1, keepdims=True)
        marks = ((lanes.astype(F32) == mark) & (lanes > 0)).astype(BF16)
        by_head(c, 0, marks)
        for t in range(3):
            by_head(c, 1 + t, rcv1[pl.ds(c * peers, peers), t].reshape(rows, dh))
        return carry

    lax.fori_loop(0, chunks, split_heads, 0)

    def cell(index, h):
        return cells[index, h].reshape(recv_rows, dh)

    def forward(h, carry):
        marks = cell(0, h)
        same = dot(marks, marks, NT) > 0.5
        scores = jnp.where(same, dot(cell(1, h), cell(2, h), NT) * scale, -1e30)
        weights = jnp.exp(scores - jnp.max(scores, axis=1, keepdims=True))
        prob = weights / jnp.sum(weights, axis=1, keepdims=True)
        probs[h] = prob
        outs[0, h] = (
            dot(prob.astype(BF16), cell(3, h)).astype(BF16).reshape(chunks, part, dh)
        )
        return carry

    lax.fori_loop(0, heads, forward, 0)

    def by_peer(c, index):
        return (
            dot(to_peers, outs[index, :, c].reshape(rows, dh))
            .astype(BF16)
            .reshape(peers, blk, dh)
        )

    def return_attended(c, carry):
        snda[pl.ds(c * peers, peers)] = by_peer(c, 0)
        return carry

    lax.fori_loop(0, chunks, return_attended, 0)
    exchange(snda, rcva, 7)
    rcva[me] = snda[me]

    wait_recv(rcvg.at[pl.ds(0, ns - 1)], 6)

    def split_grad(c, carry):
        by_head(c, 4, rcvg[pl.ds(c * peers, peers)].reshape(rows, dh))
        return carry

    lax.fori_loop(0, chunks, split_grad, 0)

    def backward(h, carry):
        grads = cell(4, h)
        prob = probs[h]
        attended = outs[0, h].reshape(recv_rows, dh)
        delta = jnp.sum(grads.astype(F32) * attended.astype(F32), axis=1, keepdims=True)
        grad_value = dot(prob.astype(BF16), grads, TN)
        grad_probs = dot(grads, cell(3, h), NT)
        grad_scores = (prob * (grad_probs - delta)).astype(BF16)
        grad_query = dot(grad_scores, cell(2, h)) * scale
        grad_key = dot(grad_scores, cell(1, h), TN) * scale
        for t, value in enumerate((grad_query, grad_key, grad_value)):
            outs[1 + t, h] = value.astype(BF16).reshape(chunks, part, dh)
        return carry

    lax.fori_loop(0, heads, backward, 0)

    def return_grads(c, carry):
        for t in range(3):
            sndb[pl.ds(c * peers, peers), t] = by_peer(c, 1 + t)
        return carry

    lax.fori_loop(0, chunks, return_grads, 0)
    exchange(sndb, rcvb, 8)
    rcvb[me] = sndb[me]

    wait_recv(rcva.at[pl.ds(0, ns - 1)], 7)
    arrived = rcva[...].reshape(ns * blk, dh)
    attended = jnp.concatenate(
        [dot(unpack[h], arrived).astype(BF16) for h in range(heads)], axis=1
    )

    def project(y, carry):
        rsnd[:, y] = (
            dot(attended, wt[y].reshape(columns, heads * dh), NT)
            .astype(BF16)
            .reshape(nt, tok // nt, columns)
        )
        return carry

    lax.fori_loop(0, ny, project, 0)

    def scatter(j, carry):
        target = lax.rem(mt + j, nt)
        remote(rsnd.at[target], rrcv.at[mt], 9, {"tensor": target}).start()
        return carry

    lax.fori_loop(1, nt, scatter, 0)
    rrcv[mt] = rsnd[mt]
    wait_recv(rrcv.at[pl.ds(0, nt - 1)], 9)
    for y in range(ny):
        total = rrcv[0, y].astype(F32)
        for t in range(1, nt):
            total = total + rrcv[t, y].astype(F32)
        mixed_ref[:, y * columns : (y + 1) * columns] = total.astype(BF16)

    wait_recv(rcvb.at[pl.ds(0, ns - 1)], 8)
    for t, ref in enumerate((dq_ref, dk_ref, dv_ref)):
        back = rcvb[:, t].reshape(ns * blk, dh)
        for h in range(heads):
            ref[:, h * dh : (h + 1) * dh] = dot(unpack[h], back).astype(BF16)

    wait_send(wt.at[pl.ds(0, ny - 1), 0, 0], 0)
    wait_send(wt.at[:, pl.ds(0, nx - 1), 0], 1)
    wait_send(wt.at[:, :, 0], 2)
    wait_send(gout.at[pl.ds(0, nt - 1)], 3)
    wait_send(msnd.at[pl.ds(0, ns - 1)], 4)
    wait_send(snd1.at[pl.ds(0, ns - 1)], 5)
    wait_send(sndg.at[pl.ds(0, ns - 1)], 6)
    wait_send(snda.at[pl.ds(0, ns - 1)], 7)
    wait_send(sndb.at[pl.ds(0, ns - 1)], 8)
    wait_send(rsnd.at[pl.ds(0, nt - 1)], 9)


def solution(mesh, grid=(8, 4)):
    ny, nx = grid
    ns, nt = mesh.shape["seq"], mesh.shape["tensor"]

    def shards(query_rows, key_rows, value_rows, cluster_id, slot_index, out_weight, grad_out):
        tok = query_rows.shape[0]
        heads = cluster_id.shape[0]
        dh = query_rows.shape[1] // heads
        blk = heads * SLOTS
        peers = min(16, ns)
        chunks = ns // peers
        rows = peers * blk
        part = peers * SLOTS
        columns = nx * 2 * 32
        vmem = pl.BlockSpec(memory_space=pltpu.VMEM)
        wide = jax.ShapeDtypeStruct(query_rows.shape, BF16)
        one = pltpu.VMEM((ns, blk, dh), BF16)
        three = pltpu.VMEM((ns, 3, blk, dh), BF16)
        return pl.pallas_call(
            functools.partial(kernel, (ny, nx, nt, heads, tok, dh)),
            out_shape=(jax.ShapeDtypeStruct(grad_out.shape, BF16), wide, wide, wide),
            in_specs=[vmem] * 6,
            out_specs=(vmem,) * 4,
            scratch_shapes=[
                pltpu.VMEM((heads * tok, 3 * dh), BF16),
                pltpu.VMEM((chunks, rows, heads * tok), BF16),
                pltpu.VMEM((heads, tok, ns * blk), BF16),
                pltpu.VMEM((ns, 1, 128), F32),
                pltpu.VMEM((ns, 1, 128), F32),
                three,
                three,
                one,
                one,
                one,
                one,
                three,
                three,
                pltpu.VMEM((ny, nx, 2, 32, heads * dh), BF16),
                pltpu.VMEM((nt,) + grad_out.shape, BF16),
                pltpu.VMEM((nt, ny, tok // nt, columns), BF16),
                pltpu.VMEM((nt, ny, tok // nt, columns), BF16),
                pltpu.VMEM((5, heads, chunks, part, dh), BF16),
                pltpu.VMEM((heads, ns * SLOTS, ns * SLOTS), F32),
                pltpu.VMEM((4, heads, chunks, part, dh), BF16),
                pltpu.SemaphoreType.DMA((10,)),
                pltpu.SemaphoreType.DMA((10,)),
            ],
            compiler_params=pltpu.CompilerParams(
                collective_id=0, has_side_effects=True, vmem_limit_bytes=48 * 1024 * 1024
            ),
        )(query_rows, key_rows, value_rows, cluster_id, out_weight, grad_out)

    return jax.shard_map(
        shards,
        mesh=mesh,
        in_specs=(
            P("seq", "tensor"),
            P("seq", "tensor"),
            P("seq", "tensor"),
            P("tensor", "seq"),
            P("tensor", "seq"),
            P("tensor", "seq"),
            P(("seq", "tensor"), None),
        ),
        out_specs=(
            P(("seq", "tensor"), None),
            P("seq", "tensor"),
            P("seq", "tensor"),
            P("seq", "tensor"),
        ),
        check_vma=False,
    )
```

```python
import functools
import math

import jax
import jax.numpy as jnp
from jax import lax
from jax.experimental import pallas as pl
from jax.experimental.pallas import tpu as pltpu
from jax.sharding import PartitionSpec as P

CLU_DEV = 8
SLOTS = 4
MESH = pl.DeviceIdType.MESH
F32 = jnp.float32
BF16 = jnp.bfloat16
NN = (((1,), (0,)), ((), ()))
NT = (((1,), (1,)), ((), ()))
TN = (((0,), (0,)), ((), ()))


def dot(a, b, dims=NN):
    return lax.dot_general(a, b, dims, preferred_element_type=F32)


def iota(shape, dim):
    return lax.broadcasted_iota(jnp.int32, shape, dim)


def kernel(
    dims,
    q_hbm,
    k_hbm,
    v_hbm,
    cid_hbm,
    w_hbm,
    go_hbm,
    mixed_ref,
    dq_ref,
    dk_ref,
    dv_ref,
    cid_ref,
    w_ref,
    xcat,
    pack,
    unpack,
    msnd,
    mrcv,
    snd1,
    rcv1,
    sndg,
    rcvg,
    snda,
    rcva,
    sndb,
    rcvb,
    grads_in,
    wt,
    gout,
    rsnd,
    rrcv,
    cells,
    probs,
    outs,
    ssem,
    rsem,
    lsem,
):
    ny, nx, nt, heads, tok, dh = dims
    ns = ny * nx * 2
    hb = heads // 2
    blk = hb * SLOTS
    peers = min(32, ns)
    chunks = ns // peers
    rows = peers * blk
    part = peers * SLOTS
    recv_rows = ns * SLOTS
    half = hb * dh
    columns = nx * 2 * 32
    scale = 1.0 / math.sqrt(dh)
    me = lax.axis_index("seq")
    mt = lax.axis_index("tensor")
    my = lax.div(me, 2 * nx)
    mx = lax.rem(lax.div(me, 2), nx)
    mc = lax.rem(me, 2)

    loads = [
        pltpu.make_async_copy(cid_hbm, cid_ref, lsem.at[0]),
        pltpu.make_async_copy(w_hbm, w_ref, lsem.at[1]),
        pltpu.make_async_copy(go_hbm, gout.at[mt], lsem.at[2]),
    ]
    for t, ref in enumerate((q_hbm, k_hbm, v_hbm)):
        for h in range(heads):
            loads.append(
                pltpu.make_async_copy(
                    ref.at[:, pl.ds(h * dh, dh)],
                    xcat.at[h // hb, pl.ds(h % hb * tok, tok), pl.ds(t * dh, dh)],
                    lsem.at[3 + t * heads + h],
                )
            )
    for load in loads:
        load.start()

    barrier = pltpu.get_barrier_semaphore()

    def greet_seq(j, carry):
        pl.semaphore_signal(
            barrier, inc=1, device_id={"seq": lax.rem(me + j, ns)}, device_id_type=MESH
        )
        return carry

    lax.fori_loop(1, ns, greet_seq, 0)

    def greet_tensor(j, carry):
        pl.semaphore_signal(
            barrier, inc=1, device_id={"tensor": lax.rem(mt + j, nt)}, device_id_type=MESH
        )
        return carry

    lax.fori_loop(1, nt, greet_tensor, 0)

    def remote(src, dst, index, target):
        return pltpu.make_async_remote_copy(
            src_ref=src,
            dst_ref=dst,
            send_sem=ssem.at[index],
            recv_sem=rsem.at[index],
            device_id=target,
            device_id_type=MESH,
        )

    def wait_recv(ref, index):
        pltpu.make_async_copy(ref, ref, rsem.at[index]).wait()

    def wait_send(ref, index):
        pltpu.make_async_copy(ref, ref, ssem.at[index]).wait()

    def exchange(src, dst, index):
        def step(j, carry):
            ahead = lax.rem(me + j, ns)
            behind = lax.rem(me + ns - j, ns)
            remote(src.at[ahead], dst.at[me], index, {"seq": ahead}).start()
            remote(src.at[behind], dst.at[me], index, {"seq": behind}).start()
            return carry

        far = lax.rem(me + ns // 2, ns)
        remote(src.at[far], dst.at[me], index, {"seq": far}).start()
        lax.fori_loop(1, ns // 2, step, 0)

    def send_rows(snd, rcv, i, index):
        exchange(snd.at[i], rcv.at[i], index + i)
        rcv[i, me] = snd[i, me]

    def wait_rows(rcv, i, index):
        wait_recv(rcv.at[i, pl.ds(0, ns - 1)], index + i)

    def flat(block):
        return block.astype(F32).reshape(-1, dh).astype(BF16)

    def tiles(values):
        return values.reshape(-1, blk, dh).astype(BF16)

    loads[0].wait()
    upper = (iota((tok, tok), 0) < iota((tok, tok), 1)).astype(BF16)
    diag = iota((tok, tok), 0) == iota((tok, tok), 1)
    table = jnp.zeros((ns, 128), F32)
    dests = []
    for h in range(heads):
        cid = cid_ref[h : h + 1, :]
        owner = lax.shift_right_logical(cid, 3)
        member = iota((ns, tok), 0) == owner
        onehot = member.astype(F32)
        earlier = dot(onehot.astype(BF16), upper)
        rank = jnp.sum(onehot * earlier, axis=0, keepdims=True).astype(jnp.int32)
        i, g = divmod(h, hb)
        dest = owner * blk + g * SLOTS + rank
        dests.append(dest)
        for c in range(chunks):
            pack[i, c, :, g * tok : (g + 1) * tok] = (
                iota((rows, tok), 0) + c * rows == dest
            ).astype(BF16)
        value = jnp.where(member, (cid & (CLU_DEV - 1)) + 1, 0).astype(F32).astype(BF16)
        lane = (iota((128, tok), 0) == rank + h * SLOTS).astype(BF16)
        table = table + dot(value, lane, NT)
    msnd[...] = table.reshape(ns, 1, 128)

    loads[1].wait()
    block = dot((iota((32, 32), 0) == iota((32, 32), 1)).astype(BF16), w_ref[...], NT)
    for i in range(2):
        wt[i, my, mx, mc] = block[:, i * half : (i + 1) * half].astype(BF16)

    for i in range(2):
        for t in range(3):
            for h in range(i * hb, (i + 1) * hb):
                loads[3 + t * heads + h].wait()
        for c in range(chunks):
            packed = dot(pack[i, c], xcat[i])
            for t in range(3):
                snd1[i, c * peers : (c + 1) * peers, t] = tiles(packed[:, t * dh : (t + 1) * dh])
    loads[2].wait()

    pl.semaphore_wait(barrier, ns - 1 + nt - 1)

    def weight_y(i):
        def step(j, carry):
            target = (lax.rem(my + j, ny) * nx + mx) * 2 + mc
            remote(
                wt.at[i, my, mx, mc], wt.at[i, my, mx, mc], 8 + i, {"seq": target}
            ).start()
            return carry

        lax.fori_loop(1, ny, step, 0)

    def weight_x(i):
        wait_recv(wt.at[i, pl.ds(0, ny - 1), 0, 0], 8 + i)

        def step(j, carry):
            target = (my * nx + lax.rem(mx + j, nx)) * 2 + mc
            remote(wt.at[i, :, mx, mc], wt.at[i, :, mx, mc], 10 + i, {"seq": target}).start()
            return carry

        lax.fori_loop(1, nx, step, 0)

    def weight_core(i):
        wait_recv(wt.at[i, :, pl.ds(0, nx - 1), 0], 10 + i)
        remote(
            wt.at[i, :, :, mc], wt.at[i, :, :, mc], 12 + i, {"seq": me + 1 - 2 * mc}
        ).start()

    weight_y(0)
    weight_y(1)

    def cotangent(j, carry):
        remote(gout.at[mt], gout.at[mt], 14, {"tensor": lax.rem(mt + j, nt)}).start()
        return carry

    lax.fori_loop(1, nt, cotangent, 0)

    exchange(msnd, mrcv, 15)
    mrcv[me] = msnd[me]
    send_rows(snd1, rcv1, 0, 0)
    weight_x(0)
    weight_x(1)
    send_rows(snd1, rcv1, 1, 0)

    for h in range(heads):
        column = jnp.sum(
            jnp.where(diag, dests[h], 0).astype(F32), axis=1, keepdims=True
        ).astype(jnp.int32)
        unpack[h] = (iota((tok, ns * blk), 1) == column).astype(BF16)

    def source(index):
        h = lax.div(index, part)
        rest = index - h * part
        p = lax.div(rest, SLOTS)
        return p * blk + h * SLOTS + (rest - p * SLOTS)

    to_heads = (source(iota((rows, 1), 0)) == iota((rows, rows), 1)).astype(BF16)
    to_peers = (source(iota((1, rows), 1)) == iota((rows, rows), 0)).astype(BF16)
    lanes = iota((rows, 128), 1)

    def grad_rows(i):
        wait_recv(wt.at[i, :, :, 0], 12 + i)
        grad = jnp.zeros((tok, half), F32)
        for y in range(ny):
            grad = grad + dot(
                gout[:, :, y * columns : (y + 1) * columns].reshape(tok, columns),
                wt[i, y].reshape(columns, half),
            )
        grad = grad.astype(BF16)
        for g in range(hb):
            grads_in[i, g * tok : (g + 1) * tok] = grad[:, g * dh : (g + 1) * dh]
        for c in range(chunks):
            sndg[i, c * peers : (c + 1) * peers] = tiles(dot(pack[i, c], grads_in[i]))
        send_rows(sndg, rcvg, i, 2)

    def by_head(i, c, values, slots):
        moved = dot(to_heads, values).astype(BF16)
        for n, slot in enumerate(slots):
            for g in range(hb):
                cells[slot, i * hb + g, c] = moved[
                    g * part : (g + 1) * part, n * dh : (n + 1) * dh
                ]

    def cell(index, h):
        return cells[index, h].reshape(recv_rows, dh)

    def keep(index, h, value):
        outs[index, h] = value.astype(BF16).reshape(chunks, part, dh)

    def by_peer(i, c, indices):
        return dot(
            to_peers,
            jnp.concatenate(
                [
                    jnp.concatenate([outs[n, i * hb + g, c] for g in range(hb)], axis=0)
                    for n in indices
                ],
                axis=1,
            ),
        )

    def forward(i):
        wait_rows(rcv1, i, 0)
        for c in range(chunks):
            here = slice(c * peers, (c + 1) * peers)
            spread = jnp.broadcast_to(mrcv[here], (peers, blk, 128)).reshape(rows, 128)
            own_lane = lanes == (iota((rows, 128), 0) & (blk - 1)) + i * blk
            mark = jnp.sum(jnp.where(own_lane, spread, 0.0), axis=1, keepdims=True)
            marks = ((lanes.astype(F32) == mark) & (lanes > 0)).astype(BF16)
            values = [flat(rcv1[i, here, t]) for t in range(3)]
            by_head(i, c, jnp.concatenate(values + [marks], axis=1), (0, 1, 2, 4))
        for h in range(i * hb, (i + 1) * hb):
            marks = cell(4, h)
            same = dot(marks, marks, NT) > 0.5
            scores = jnp.where(same, dot(cell(0, h), cell(1, h), NT) * scale, -1e30)
            weights = jnp.exp(scores - jnp.max(scores, axis=1, keepdims=True))
            prob = weights / jnp.sum(weights, axis=1, keepdims=True)
            probs[h] = prob
            keep(0, h, dot(prob.astype(BF16), cell(2, h)))
        for c in range(chunks):
            snda[i, c * peers : (c + 1) * peers] = tiles(by_peer(i, c, (0,)))
        send_rows(snda, rcva, i, 4)

    def backward(i):
        wait_rows(rcvg, i, 2)
        for c in range(chunks):
            by_head(i, c, flat(rcvg[i, c * peers : (c + 1) * peers]), (3,))
        for h in range(i * hb, (i + 1) * hb):
            grads = cell(3, h)
            prob = probs[h]
            attended = outs[0, h].reshape(recv_rows, dh)
            delta = jnp.sum(grads.astype(F32) * attended.astype(F32), axis=1, keepdims=True)
            grad_probs = dot(grads, cell(2, h), NT)
            grad_scores = (prob * (grad_probs - delta)).astype(BF16)
            keep(1, h, dot(grad_scores, cell(1, h)) * scale)
            keep(2, h, dot(grad_scores, cell(0, h), TN) * scale)
            keep(3, h, dot(prob.astype(BF16), grads, TN))
        for c in range(chunks):
            back = by_peer(i, c, (1, 2, 3))
            for t in range(3):
                sndb[i, c * peers : (c + 1) * peers, t] = tiles(back[:, t * dh : (t + 1) * dh])
        send_rows(sndb, rcvb, i, 6)

    weight_core(0)
    wait_recv(gout.at[pl.ds(0, nt - 1)], 14)
    grad_rows(0)
    weight_core(1)
    wait_recv(mrcv.at[pl.ds(0, ns - 1)], 15)
    forward(0)
    grad_rows(1)
    forward(1)
    backward(0)
    backward(1)

    attended = []
    for i in range(2):
        wait_rows(rcva, i, 4)
        arrived = flat(rcva[i])
        attended.append(
            jnp.concatenate(
                [dot(unpack[h], arrived).astype(BF16) for h in range(i * hb, (i + 1) * hb)],
                axis=1,
            )
        )

    def project(y, carry):
        rsnd[:, y] = (
            (
                dot(attended[0], wt[0, y].reshape(columns, half), NT)
                + dot(attended[1], wt[1, y].reshape(columns, half), NT)
            )
            .astype(BF16)
            .reshape(nt, tok // nt, columns)
        )

        def scatter(j, inner):
            target = lax.rem(mt + j, nt)
            remote(rsnd.at[target, y], rrcv.at[mt, y], 16, {"tensor": target}).start()
            return inner

        lax.fori_loop(1, nt, scatter, 0)
        rrcv[mt, y] = rsnd[mt, y]
        return carry

    lax.fori_loop(0, ny, project, 0)

    def deliver(i):
        wait_rows(rcvb, i, 6)
        arrived = jnp.concatenate([flat(rcvb[i, :, t]) for t in range(3)], axis=1)
        for h in range(i * hb, (i + 1) * hb):
            back = dot(unpack[h], arrived).astype(BF16)
            for t, ref in enumerate((dq_ref, dk_ref, dv_ref)):
                ref[:, h * dh : (h + 1) * dh] = back[:, t * dh : (t + 1) * dh]

    deliver(0)
    wait_recv(rrcv.at[pl.ds(0, nt - 1)], 16)
    for y in range(ny):
        total = rrcv[0, y].astype(F32)
        for t in range(1, nt):
            total = total + rrcv[t, y].astype(F32)
        mixed_ref[:, y * columns : (y + 1) * columns] = total.astype(BF16)
    deliver(1)

    for i in range(2):
        wait_send(wt.at[i, pl.ds(0, ny - 1), 0, 0], 8 + i)
        wait_send(wt.at[i, :, pl.ds(0, nx - 1), 0], 10 + i)
        wait_send(wt.at[i, :, :, 0], 12 + i)
    wait_send(gout.at[pl.ds(0, nt - 1)], 14)
    wait_send(msnd.at[pl.ds(0, ns - 1)], 15)
    wait_send(rsnd.at[pl.ds(0, nt - 1)], 16)
    for i in range(2):
        for n, ref in enumerate((snd1, sndg, snda, sndb)):
            wait_send(ref.at[i, pl.ds(0, ns - 1)], 2 * n + i)


def solution(mesh, grid=(8, 4)):
    ny, nx = grid
    ns, nt = mesh.shape["seq"], mesh.shape["tensor"]

    def shards(query_rows, key_rows, value_rows, cluster_id, slot_index, out_weight, grad_out):
        tok = query_rows.shape[0]
        heads = cluster_id.shape[0]
        dh = query_rows.shape[1] // heads
        hb = heads // 2
        blk = hb * SLOTS
        peers = min(32, ns)
        chunks = ns // peers
        rows = peers * blk
        part = peers * SLOTS
        columns = nx * 2 * 32
        vmem = pl.BlockSpec(memory_space=pltpu.VMEM)
        one = pltpu.VMEM((2, ns, blk, dh), BF16)
        three = pltpu.VMEM((2, ns, 3, blk, dh), BF16)
        wide = jax.ShapeDtypeStruct(query_rows.shape, BF16)
        return pl.pallas_call(
            functools.partial(kernel, (ny, nx, nt, heads, tok, dh)),
            out_shape=(jax.ShapeDtypeStruct(grad_out.shape, BF16), wide, wide, wide),
            in_specs=[pl.BlockSpec(memory_space=pltpu.HBM)] * 6,
            out_specs=(vmem,) * 4,
            scratch_shapes=[
                pltpu.VMEM(cluster_id.shape, jnp.int32),
                pltpu.VMEM(out_weight.shape, BF16),
                pltpu.VMEM((2, hb * tok, 3 * dh), BF16),
                pltpu.VMEM((2, chunks, rows, hb * tok), BF16),
                pltpu.VMEM((heads, tok, ns * blk), BF16),
                pltpu.VMEM((ns, 1, 128), F32),
                pltpu.VMEM((ns, 1, 128), F32),
                three,
                three,
                one,
                one,
                one,
                one,
                three,
                three,
                pltpu.VMEM((2, hb * tok, dh), BF16),
                pltpu.VMEM((2, ny, nx, 2, 32, heads * dh // 2), BF16),
                pltpu.VMEM((nt,) + grad_out.shape, BF16),
                pltpu.VMEM((nt, ny, tok // nt, columns), BF16),
                pltpu.VMEM((nt, ny, tok // nt, columns), BF16),
                pltpu.VMEM((5, heads, chunks, part, dh), BF16),
                pltpu.VMEM((heads, ns * SLOTS, ns * SLOTS), F32),
                pltpu.VMEM((4, heads, chunks, part, dh), BF16),
                pltpu.SemaphoreType.DMA((17,)),
                pltpu.SemaphoreType.DMA((17,)),
                pltpu.SemaphoreType.DMA((3 + 3 * heads,)),
            ],
            compiler_params=pltpu.CompilerParams(
                collective_id=0, has_side_effects=True, vmem_limit_bytes=48 * 1024 * 1024
            ),
        )(query_rows, key_rows, value_rows, cluster_id, out_weight, grad_out)

    return jax.shard_map(
        shards,
        mesh=mesh,
        in_specs=(
            P("seq", "tensor"),
            P("seq", "tensor"),
            P("seq", "tensor"),
            P("tensor", "seq"),
            P("tensor", "seq"),
            P("tensor", "seq"),
            P(("seq", "tensor"), None),
        ),
        out_specs=(
            P(("seq", "tensor"), None),
            P("seq", "tensor"),
            P("seq", "tensor"),
            P("seq", "tensor"),
        ),
        check_vma=False,
    )
```

```python
import functools
import math

import jax
import jax.numpy as jnp
from jax import lax
from jax.experimental import pallas as pl
from jax.experimental.pallas import tpu as pltpu
from jax.sharding import PartitionSpec as P

CLU_DEV = 8
SLOTS = 4
MESH = pl.DeviceIdType.MESH
F32 = jnp.float32
BF16 = jnp.bfloat16
NN = (((1,), (0,)), ((), ()))
NT = (((1,), (1,)), ((), ()))
TN = (((0,), (0,)), ((), ()))


def dot(a, b, dims=NN):
    return lax.dot_general(a, b, dims, preferred_element_type=F32)


def iota(shape, dim):
    return lax.broadcasted_iota(jnp.int32, shape, dim)


def kernel(
    dims,
    q_hbm,
    k_hbm,
    v_hbm,
    cid_hbm,
    w_hbm,
    go_hbm,
    mixed_ref,
    dq_ref,
    dk_ref,
    dv_ref,
    cid_ref,
    w_ref,
    xcat,
    pack,
    unpack,
    msnd,
    mrcv,
    snd1,
    rcv1,
    sndg,
    rcvg,
    snda,
    rcva,
    sndb,
    rcvb,
    grads_in,
    wt,
    gout,
    rsnd,
    rrcv,
    cells,
    probs,
    outs,
    ssem,
    rsem,
    lsem,
):
    ny, nx, nt, heads, tok, dh = dims
    ns = ny * nx * 2
    hb = heads // 2
    blk = hb * SLOTS
    peers = min(32, ns)
    chunks = ns // peers
    rows = peers * blk
    part = peers * SLOTS
    recv_rows = ns * SLOTS
    half = hb * dh
    columns = nx * 2 * 32
    scale = 1.0 / math.sqrt(dh)
    me = lax.axis_index("seq")
    mt = lax.axis_index("tensor")
    my = lax.div(me, 2 * nx)
    mx = lax.rem(lax.div(me, 2), nx)
    mc = lax.rem(me, 2)

    loads = [
        pltpu.make_async_copy(cid_hbm, cid_ref, lsem.at[0]),
        pltpu.make_async_copy(w_hbm, w_ref, lsem.at[1]),
        pltpu.make_async_copy(go_hbm, gout.at[mt], lsem.at[2]),
    ]
    for t, ref in enumerate((q_hbm, k_hbm, v_hbm)):
        for h in range(heads):
            loads.append(
                pltpu.make_async_copy(
                    ref.at[:, pl.ds(h * dh, dh)],
                    xcat.at[h // hb, pl.ds(h % hb * tok, tok), pl.ds(t * dh, dh)],
                    lsem.at[3 + t * heads + h],
                )
            )
    for load in loads:
        load.start()

    barrier = pltpu.get_barrier_semaphore()

    def greet_seq(j, carry):
        pl.semaphore_signal(
            barrier, inc=1, device_id={"seq": lax.rem(me + j, ns)}, device_id_type=MESH
        )
        return carry

    lax.fori_loop(1, ns, greet_seq, 0)

    def greet_tensor(j, carry):
        pl.semaphore_signal(
            barrier, inc=1, device_id={"tensor": lax.rem(mt + j, nt)}, device_id_type=MESH
        )
        return carry

    lax.fori_loop(1, nt, greet_tensor, 0)

    def remote(src, dst, index, target):
        return pltpu.make_async_remote_copy(
            src_ref=src,
            dst_ref=dst,
            send_sem=ssem.at[index],
            recv_sem=rsem.at[index],
            device_id=target,
            device_id_type=MESH,
        )

    def wait_recv(ref, index):
        pltpu.make_async_copy(ref, ref, rsem.at[index]).wait()

    def wait_send(ref, index):
        pltpu.make_async_copy(ref, ref, ssem.at[index]).wait()

    def exchange(src, dst, index):
        def step(j, carry):
            ahead = lax.rem(me + j, ns)
            behind = lax.rem(me + ns - j, ns)
            remote(src.at[ahead], dst.at[me], index, {"seq": ahead}).start()
            remote(src.at[behind], dst.at[me], index, {"seq": behind}).start()
            return carry

        far = lax.rem(me + ns // 2, ns)
        remote(src.at[far], dst.at[me], index, {"seq": far}).start()
        lax.fori_loop(1, ns // 2, step, 0)

    def send_rows(snd, rcv, i, index):
        exchange(snd.at[i], rcv.at[i], index + i)
        rcv[i, me] = snd[i, me]

    def wait_rows(rcv, i, index):
        wait_recv(rcv.at[i, pl.ds(0, ns - 1)], index + i)

    def flat(block):
        return block.astype(F32).reshape(-1, dh).astype(BF16)

    def tiles(values):
        return values.reshape(-1, blk, dh).astype(BF16)

    loads[0].wait()
    upper = (iota((tok, tok), 0) < iota((tok, tok), 1)).astype(BF16)
    diag = iota((tok, tok), 0) == iota((tok, tok), 1)
    table = jnp.zeros((ns, 128), F32)
    dests = []
    for h in range(heads):
        cid = cid_ref[h : h + 1, :]
        owner = lax.shift_right_logical(cid, 3)
        member = iota((ns, tok), 0) == owner
        onehot = member.astype(F32)
        earlier = dot(onehot.astype(BF16), upper)
        rank = jnp.sum(onehot * earlier, axis=0, keepdims=True).astype(jnp.int32)
        i, g = divmod(h, hb)
        dest = owner * blk + g * SLOTS + rank
        dests.append(dest)
        for c in range(chunks):
            pack[i, c, :, g * tok : (g + 1) * tok] = (
                iota((rows, tok), 0) + c * rows == dest
            ).astype(BF16)
        value = jnp.where(member, (cid & (CLU_DEV - 1)) + 1, 0).astype(F32).astype(BF16)
        lane = (iota((128, tok), 0) == rank + h * SLOTS).astype(BF16)
        table = table + dot(value, lane, NT)
    msnd[...] = table.reshape(ns, 1, 128)

    loads[1].wait()
    block = dot((iota((32, 32), 0) == iota((32, 32), 1)).astype(BF16), w_ref[...], NT)
    for i in range(2):
        wt[i, my, mx, mc] = block[:, i * half : (i + 1) * half].astype(BF16)

    for i in range(2):
        for t in range(3):
            for h in range(i * hb, (i + 1) * hb):
                loads[3 + t * heads + h].wait()
        for c in range(chunks):
            packed = dot(pack[i, c], xcat[i])
            for t in range(3):
                snd1[i, c * peers : (c + 1) * peers, t] = tiles(packed[:, t * dh : (t + 1) * dh])
    loads[2].wait()

    pl.semaphore_wait(barrier, ns - 1 + nt - 1)

    def weight_y(i):
        def step(j, carry):
            target = (lax.rem(my + j, ny) * nx + mx) * 2 + mc
            remote(
                wt.at[i, my, mx, mc], wt.at[i, my, mx, mc], 8 + i, {"seq": target}
            ).start()
            return carry

        lax.fori_loop(1, ny, step, 0)

    def weight_x(i):
        wait_recv(wt.at[i, pl.ds(0, ny - 1), 0, 0], 8 + i)

        def step(j, carry):
            target = (my * nx + lax.rem(mx + j, nx)) * 2 + mc
            remote(wt.at[i, :, mx, mc], wt.at[i, :, mx, mc], 10 + i, {"seq": target}).start()
            return carry

        lax.fori_loop(1, nx, step, 0)

    def weight_core(i):
        wait_recv(wt.at[i, :, pl.ds(0, nx - 1), 0], 10 + i)
        remote(
            wt.at[i, :, :, mc], wt.at[i, :, :, mc], 12 + i, {"seq": me + 1 - 2 * mc}
        ).start()

    weight_y(0)
    weight_y(1)

    def cotangent(j, carry):
        remote(gout.at[mt], gout.at[mt], 14, {"tensor": lax.rem(mt + j, nt)}).start()
        return carry

    lax.fori_loop(1, nt, cotangent, 0)

    exchange(msnd, mrcv, 15)
    mrcv[me] = msnd[me]
    send_rows(snd1, rcv1, 0, 0)
    send_rows(snd1, rcv1, 1, 0)
    weight_x(0)
    weight_x(1)

    for h in range(heads):
        column = jnp.sum(
            jnp.where(diag, dests[h], 0).astype(F32), axis=1, keepdims=True
        ).astype(jnp.int32)
        unpack[h] = (iota((tok, ns * blk), 1) == column).astype(BF16)

    def source(index):
        h = lax.div(index, part)
        rest = index - h * part
        p = lax.div(rest, SLOTS)
        return p * blk + h * SLOTS + (rest - p * SLOTS)

    to_heads = (source(iota((rows, 1), 0)) == iota((rows, rows), 1)).astype(BF16)
    to_peers = (source(iota((1, rows), 1)) == iota((rows, rows), 0)).astype(BF16)
    lanes = iota((rows, 128), 1)

    def grad_rows(i):
        wait_recv(wt.at[i, :, :, 0], 12 + i)
        grad = jnp.zeros((tok, half), F32)
        for y in range(ny):
            grad = grad + dot(
                gout[:, :, y * columns : (y + 1) * columns].reshape(tok, columns),
                wt[i, y].reshape(columns, half),
            )
        grad = grad.astype(BF16)
        for g in range(hb):
            grads_in[i, g * tok : (g + 1) * tok] = grad[:, g * dh : (g + 1) * dh]
        for c in range(chunks):
            sndg[i, c * peers : (c + 1) * peers] = tiles(dot(pack[i, c], grads_in[i]))
        send_rows(sndg, rcvg, i, 2)

    def by_head(i, c, values, slots):
        moved = dot(to_heads, values).astype(BF16)
        for n, slot in enumerate(slots):
            for g in range(hb):
                cells[slot, i * hb + g, c] = moved[
                    g * part : (g + 1) * part, n * dh : (n + 1) * dh
                ]

    def cell(index, h):
        return cells[index, h].reshape(recv_rows, dh)

    def keep(index, h, value):
        outs[index, h] = value.astype(BF16).reshape(chunks, part, dh)

    def by_peer(i, c, indices):
        return dot(
            to_peers,
            jnp.concatenate(
                [
                    jnp.concatenate([outs[n, i * hb + g, c] for g in range(hb)], axis=0)
                    for n in indices
                ],
                axis=1,
            ),
        )

    def forward(i):
        wait_rows(rcv1, i, 0)
        for c in range(chunks):
            here = slice(c * peers, (c + 1) * peers)
            spread = jnp.broadcast_to(mrcv[here], (peers, blk, 128)).reshape(rows, 128)
            own_lane = lanes == (iota((rows, 128), 0) & (blk - 1)) + i * blk
            mark = jnp.sum(jnp.where(own_lane, spread, 0.0), axis=1, keepdims=True)
            marks = ((lanes.astype(F32) == mark) & (lanes > 0)).astype(BF16)
            values = [flat(rcv1[i, here, t]) for t in range(3)]
            by_head(i, c, jnp.concatenate(values + [marks], axis=1), (0, 1, 2, 4))
        for h in range(i * hb, (i + 1) * hb):
            marks = cell(4, h)
            same = dot(marks, marks, NT) > 0.5
            scores = jnp.where(same, dot(cell(0, h), cell(1, h), NT) * scale, -1e30)
            weights = jnp.exp(scores - jnp.max(scores, axis=1, keepdims=True))
            prob = weights / jnp.sum(weights, axis=1, keepdims=True)
            probs[h] = prob
            keep(0, h, dot(prob.astype(BF16), cell(2, h)))
        for c in range(chunks):
            snda[i, c * peers : (c + 1) * peers] = tiles(by_peer(i, c, (0,)))
        send_rows(snda, rcva, i, 4)

    def backward(i):
        wait_rows(rcvg, i, 2)
        for c in range(chunks):
            by_head(i, c, flat(rcvg[i, c * peers : (c + 1) * peers]), (3,))
        for h in range(i * hb, (i + 1) * hb):
            grads = cell(3, h)
            prob = probs[h]
            attended = outs[0, h].reshape(recv_rows, dh)
            delta = jnp.sum(grads.astype(F32) * attended.astype(F32), axis=1, keepdims=True)
            grad_probs = dot(grads, cell(2, h), NT)
            grad_scores = (prob * (grad_probs - delta)).astype(BF16)
            keep(1, h, dot(grad_scores, cell(1, h)) * scale)
            keep(2, h, dot(grad_scores, cell(0, h), TN) * scale)
            keep(3, h, dot(prob.astype(BF16), grads, TN))
        for c in range(chunks):
            back = by_peer(i, c, (1, 2, 3))
            for t in range(3):
                sndb[i, c * peers : (c + 1) * peers, t] = tiles(back[:, t * dh : (t + 1) * dh])
        send_rows(sndb, rcvb, i, 6)

    weight_core(0)
    wait_recv(mrcv.at[pl.ds(0, ns - 1)], 15)
    forward(0)
    wait_recv(gout.at[pl.ds(0, nt - 1)], 14)
    grad_rows(0)
    weight_core(1)
    forward(1)
    grad_rows(1)
    backward(0)
    attended = []
    for i in range(2):
        wait_rows(rcva, i, 4)
        arrived = flat(rcva[i])
        attended.append(
            jnp.concatenate(
                [dot(unpack[h], arrived).astype(BF16) for h in range(i * hb, (i + 1) * hb)],
                axis=1,
            )
        )

    def project(y, carry):
        rsnd[:, y] = (
            (
                dot(attended[0], wt[0, y].reshape(columns, half), NT)
                + dot(attended[1], wt[1, y].reshape(columns, half), NT)
            )
            .astype(BF16)
            .reshape(nt, tok // nt, columns)
        )

        def scatter(j, inner):
            target = lax.rem(mt + j, nt)
            remote(rsnd.at[target, y], rrcv.at[mt, y], 16, {"tensor": target}).start()
            return inner

        lax.fori_loop(1, nt, scatter, 0)
        rrcv[mt, y] = rsnd[mt, y]
        return carry

    lax.fori_loop(0, ny, project, 0)

    backward(1)

    def deliver(i):
        wait_rows(rcvb, i, 6)
        arrived = jnp.concatenate([flat(rcvb[i, :, t]) for t in range(3)], axis=1)
        for h in range(i * hb, (i + 1) * hb):
            back = dot(unpack[h], arrived).astype(BF16)
            for t, ref in enumerate((dq_ref, dk_ref, dv_ref)):
                ref[:, h * dh : (h + 1) * dh] = back[:, t * dh : (t + 1) * dh]

    deliver(0)
    wait_recv(rrcv.at[pl.ds(0, nt - 1)], 16)
    for y in range(ny):
        total = rrcv[0, y].astype(F32)
        for t in range(1, nt):
            total = total + rrcv[t, y].astype(F32)
        mixed_ref[:, y * columns : (y + 1) * columns] = total.astype(BF16)
    deliver(1)

    for i in range(2):
        wait_send(wt.at[i, pl.ds(0, ny - 1), 0, 0], 8 + i)
        wait_send(wt.at[i, :, pl.ds(0, nx - 1), 0], 10 + i)
        wait_send(wt.at[i, :, :, 0], 12 + i)
    wait_send(gout.at[pl.ds(0, nt - 1)], 14)
    wait_send(msnd.at[pl.ds(0, ns - 1)], 15)
    wait_send(rsnd.at[pl.ds(0, nt - 1)], 16)
    for i in range(2):
        for n, ref in enumerate((snd1, sndg, snda, sndb)):
            wait_send(ref.at[i, pl.ds(0, ns - 1)], 2 * n + i)


def solution(mesh, grid=(8, 4)):
    ny, nx = grid
    ns, nt = mesh.shape["seq"], mesh.shape["tensor"]

    def shards(query_rows, key_rows, value_rows, cluster_id, slot_index, out_weight, grad_out):
        tok = query_rows.shape[0]
        heads = cluster_id.shape[0]
        dh = query_rows.shape[1] // heads
        hb = heads // 2
        blk = hb * SLOTS
        peers = min(32, ns)
        chunks = ns // peers
        rows = peers * blk
        part = peers * SLOTS
        columns = nx * 2 * 32
        vmem = pl.BlockSpec(memory_space=pltpu.VMEM)
        one = pltpu.VMEM((2, ns, blk, dh), BF16)
        three = pltpu.VMEM((2, ns, 3, blk, dh), BF16)
        wide = jax.ShapeDtypeStruct(query_rows.shape, BF16)
        return pl.pallas_call(
            functools.partial(kernel, (ny, nx, nt, heads, tok, dh)),
            out_shape=(jax.ShapeDtypeStruct(grad_out.shape, BF16), wide, wide, wide),
            in_specs=[pl.BlockSpec(memory_space=pltpu.HBM)] * 6,
            out_specs=(vmem,) * 4,
            scratch_shapes=[
                pltpu.VMEM(cluster_id.shape, jnp.int32),
                pltpu.VMEM(out_weight.shape, BF16),
                pltpu.VMEM((2, hb * tok, 3 * dh), BF16),
                pltpu.VMEM((2, chunks, rows, hb * tok), BF16),
                pltpu.VMEM((heads, tok, ns * blk), BF16),
                pltpu.VMEM((ns, 1, 128), F32),
                pltpu.VMEM((ns, 1, 128), F32),
                three,
                three,
                one,
                one,
                one,
                one,
                three,
                three,
                pltpu.VMEM((2, hb * tok, dh), BF16),
                pltpu.VMEM((2, ny, nx, 2, 32, heads * dh // 2), BF16),
                pltpu.VMEM((nt,) + grad_out.shape, BF16),
                pltpu.VMEM((nt, ny, tok // nt, columns), BF16),
                pltpu.VMEM((nt, ny, tok // nt, columns), BF16),
                pltpu.VMEM((5, heads, chunks, part, dh), BF16),
                pltpu.VMEM((heads, ns * SLOTS, ns * SLOTS), F32),
                pltpu.VMEM((4, heads, chunks, part, dh), BF16),
                pltpu.SemaphoreType.DMA((17,)),
                pltpu.SemaphoreType.DMA((17,)),
                pltpu.SemaphoreType.DMA((3 + 3 * heads,)),
            ],
            compiler_params=pltpu.CompilerParams(
                collective_id=0, has_side_effects=True, vmem_limit_bytes=48 * 1024 * 1024
            ),
        )(query_rows, key_rows, value_rows, cluster_id, out_weight, grad_out)

    return jax.shard_map(
        shards,
        mesh=mesh,
        in_specs=(
            P("seq", "tensor"),
            P("seq", "tensor"),
            P("seq", "tensor"),
            P("tensor", "seq"),
            P("tensor", "seq"),
            P("tensor", "seq"),
            P(("seq", "tensor"), None),
        ),
        out_specs=(
            P(("seq", "tensor"), None),
            P("seq", "tensor"),
            P("seq", "tensor"),
            P("seq", "tensor"),
        ),
        check_vma=False,
    )
```

```python
import functools
import math

import jax
import jax.numpy as jnp
from jax import lax
from jax.experimental import pallas as pl
from jax.experimental.pallas import tpu as pltpu
from jax.sharding import PartitionSpec as P

CLU_DEV = 8
SLOTS = 4
MESH = pl.DeviceIdType.MESH
F32 = jnp.float32
BF16 = jnp.bfloat16
NN = (((1,), (0,)), ((), ()))
NT = (((1,), (1,)), ((), ()))
TN = (((0,), (0,)), ((), ()))


def dot(a, b, dims=NN):
    return lax.dot_general(a, b, dims, preferred_element_type=F32)


def iota(shape, dim):
    return lax.broadcasted_iota(jnp.int32, shape, dim)


def kernel(
    dims,
    q_hbm,
    k_hbm,
    v_hbm,
    cid_hbm,
    w_hbm,
    go_hbm,
    mixed_ref,
    dq_ref,
    dk_ref,
    dv_ref,
    cid_ref,
    w_ref,
    xcat,
    pack,
    unpack,
    msnd,
    mrcv,
    snd1,
    rcv1,
    sndg,
    rcvg,
    snda,
    rcva,
    sndb,
    rcvb,
    grads_in,
    wt,
    gout,
    rsnd,
    rrcv,
    cells,
    probs,
    outs,
    ssem,
    rsem,
    lsem,
):
    ny, nx, nt, heads, tok, dh = dims
    ns = ny * nx * 2
    hb = heads // 2
    blk = hb * SLOTS
    peers = min(32, ns)
    chunks = ns // peers
    rows = peers * blk
    part = peers * SLOTS
    recv_rows = ns * SLOTS
    half = hb * dh
    columns = nx * 2 * 32
    scale = 1.0 / math.sqrt(dh)
    me = lax.axis_index("seq")
    mt = lax.axis_index("tensor")
    my = lax.div(me, 2 * nx)
    mx = lax.rem(lax.div(me, 2), nx)
    mc = lax.rem(me, 2)

    loads = [
        pltpu.make_async_copy(cid_hbm, cid_ref, lsem.at[0]),
        pltpu.make_async_copy(w_hbm, w_ref, lsem.at[1]),
        pltpu.make_async_copy(go_hbm, gout.at[mt], lsem.at[2]),
    ]
    for t, ref in enumerate((q_hbm, k_hbm, v_hbm)):
        for h in range(heads):
            loads.append(
                pltpu.make_async_copy(
                    ref.at[:, pl.ds(h * dh, dh)],
                    xcat.at[h // hb, pl.ds(h % hb * tok, tok), pl.ds(t * dh, dh)],
                    lsem.at[3 + t * heads + h],
                )
            )
    for load in loads:
        load.start()

    barrier = pltpu.get_barrier_semaphore()

    def greet(peer):
        pl.semaphore_signal(
            barrier, inc=1, device_id={"seq": lax.rem(peer, ns)}, device_id_type=MESH
        )

    def greet_seq(j, carry):
        greet(me + ns // 2 + j)
        greet(me + ns // 2 - j)
        return carry

    greet(me + ns // 2)
    lax.fori_loop(1, ns // 2, greet_seq, 0)

    def greet_tensor(j, carry):
        pl.semaphore_signal(
            barrier, inc=1, device_id={"tensor": lax.rem(mt + j, nt)}, device_id_type=MESH
        )
        return carry

    lax.fori_loop(1, nt, greet_tensor, 0)

    def remote(src, dst, index, target):
        return pltpu.make_async_remote_copy(
            src_ref=src,
            dst_ref=dst,
            send_sem=ssem.at[index],
            recv_sem=rsem.at[index],
            device_id=target,
            device_id_type=MESH,
        )

    def wait_recv(ref, index):
        pltpu.make_async_copy(ref, ref, rsem.at[index]).wait()

    def wait_send(ref, index):
        pltpu.make_async_copy(ref, ref, ssem.at[index]).wait()

    def exchange(src, dst, index):
        def step(j, carry):
            ahead = lax.rem(me + ns // 2 + j, ns)
            behind = lax.rem(me + ns // 2 - j, ns)
            remote(src.at[ahead], dst.at[me], index, {"seq": ahead}).start()
            remote(src.at[behind], dst.at[me], index, {"seq": behind}).start()
            return carry

        far = lax.rem(me + ns // 2, ns)
        remote(src.at[far], dst.at[me], index, {"seq": far}).start()
        lax.fori_loop(1, ns // 2, step, 0)

    def send_rows(snd, rcv, i, index):
        exchange(snd.at[i], rcv.at[i], index + i)
        rcv[i, me] = snd[i, me]

    def wait_rows(rcv, i, index):
        wait_recv(rcv.at[i, pl.ds(0, ns - 1)], index + i)

    def flat(block):
        return block.astype(F32).reshape(-1, dh).astype(BF16)

    def tiles(values):
        return values.reshape(-1, blk, dh).astype(BF16)

    loads[0].wait()
    upper = (iota((tok, tok), 0) < iota((tok, tok), 1)).astype(BF16)
    diag = iota((tok, tok), 0) == iota((tok, tok), 1)
    table = jnp.zeros((ns, 128), F32)
    dests = []
    for h in range(heads):
        cid = cid_ref[h : h + 1, :]
        owner = lax.shift_right_logical(cid, 3)
        member = iota((ns, tok), 0) == owner
        onehot = member.astype(F32)
        earlier = dot(onehot.astype(BF16), upper)
        rank = jnp.sum(onehot * earlier, axis=0, keepdims=True).astype(jnp.int32)
        i, g = divmod(h, hb)
        dest = owner * blk + g * SLOTS + rank
        dests.append(dest)
        for c in range(chunks):
            pack[i, c, :, g * tok : (g + 1) * tok] = (
                iota((rows, tok), 0) + c * rows == dest
            ).astype(BF16)
        value = jnp.where(member, (cid & (CLU_DEV - 1)) + 1, 0).astype(F32).astype(BF16)
        lane = (iota((128, tok), 0) == rank + h * SLOTS).astype(BF16)
        table = table + dot(value, lane, NT)
    msnd[...] = table.reshape(ns, 1, 128)

    loads[1].wait()
    block = dot((iota((32, 32), 0) == iota((32, 32), 1)).astype(BF16), w_ref[...], NT)
    for i in range(2):
        wt[i, my, mx, mc] = block[:, i * half : (i + 1) * half].astype(BF16)

    for i in range(2):
        for t in range(3):
            for h in range(i * hb, (i + 1) * hb):
                loads[3 + t * heads + h].wait()
        for c in range(chunks):
            packed = dot(pack[i, c], xcat[i])
            for t in range(3):
                snd1[i, c * peers : (c + 1) * peers, t] = tiles(packed[:, t * dh : (t + 1) * dh])
    loads[2].wait()

    pl.semaphore_wait(barrier, ns - 1 + nt - 1)

    def weight_y(i):
        def step(j, carry):
            target = (lax.rem(my + j, ny) * nx + mx) * 2 + mc
            remote(
                wt.at[i, my, mx, mc], wt.at[i, my, mx, mc], 8 + i, {"seq": target}
            ).start()
            return carry

        lax.fori_loop(1, ny, step, 0)

    def weight_x(i):
        wait_recv(wt.at[i, pl.ds(0, ny - 1), 0, 0], 8 + i)

        def step(j, carry):
            target = (my * nx + lax.rem(mx + j, nx)) * 2 + mc
            remote(wt.at[i, :, mx, mc], wt.at[i, :, mx, mc], 10 + i, {"seq": target}).start()
            return carry

        lax.fori_loop(1, nx, step, 0)

    def weight_core(i):
        wait_recv(wt.at[i, :, pl.ds(0, nx - 1), 0], 10 + i)
        remote(
            wt.at[i, :, :, mc], wt.at[i, :, :, mc], 12 + i, {"seq": me + 1 - 2 * mc}
        ).start()

    weight_y(0)
    weight_y(1)

    def cotangent(j, carry):
        remote(gout.at[mt], gout.at[mt], 14, {"tensor": lax.rem(mt + j, nt)}).start()
        return carry

    lax.fori_loop(1, nt, cotangent, 0)

    exchange(msnd, mrcv, 15)
    mrcv[me] = msnd[me]
    send_rows(snd1, rcv1, 0, 0)
    send_rows(snd1, rcv1, 1, 0)
    weight_x(0)
    weight_x(1)

    for h in range(heads):
        column = jnp.sum(
            jnp.where(diag, dests[h], 0).astype(F32), axis=1, keepdims=True
        ).astype(jnp.int32)
        unpack[h] = (iota((tok, ns * blk), 1) == column).astype(BF16)

    def source(index):
        h = lax.div(index, part)
        rest = index - h * part
        p = lax.div(rest, SLOTS)
        return p * blk + h * SLOTS + (rest - p * SLOTS)

    to_heads = (source(iota((rows, 1), 0)) == iota((rows, rows), 1)).astype(BF16)
    to_peers = (source(iota((1, rows), 1)) == iota((rows, rows), 0)).astype(BF16)
    lanes = iota((rows, 128), 1)

    def grad_rows(i):
        wait_recv(wt.at[i, :, :, 0], 12 + i)
        grad = jnp.zeros((tok, half), F32)
        for y in range(ny):
            grad = grad + dot(
                gout[:, :, y * columns : (y + 1) * columns].reshape(tok, columns),
                wt[i, y].reshape(columns, half),
            )
        grad = grad.astype(BF16)
        for g in range(hb):
            grads_in[i, g * tok : (g + 1) * tok] = grad[:, g * dh : (g + 1) * dh]
        for c in range(chunks):
            sndg[i, c * peers : (c + 1) * peers] = tiles(dot(pack[i, c], grads_in[i]))
        send_rows(sndg, rcvg, i, 2)

    def by_head(i, c, values, slots):
        moved = dot(to_heads, values).astype(BF16)
        for n, slot in enumerate(slots):
            for g in range(hb):
                cells[slot, i * hb + g, c] = moved[
                    g * part : (g + 1) * part, n * dh : (n + 1) * dh
                ]

    def cell(index, h):
        return cells[index, h].reshape(recv_rows, dh)

    def keep(index, h, value):
        outs[index, h] = value.astype(BF16).reshape(chunks, part, dh)

    def by_peer(i, c, indices):
        return dot(
            to_peers,
            jnp.concatenate(
                [
                    jnp.concatenate([outs[n, i * hb + g, c] for g in range(hb)], axis=0)
                    for n in indices
                ],
                axis=1,
            ),
        )

    def forward(i):
        wait_rows(rcv1, i, 0)
        for c in range(chunks):
            here = slice(c * peers, (c + 1) * peers)
            spread = jnp.broadcast_to(mrcv[here], (peers, blk, 128)).reshape(rows, 128)
            own_lane = lanes == (iota((rows, 128), 0) & (blk - 1)) + i * blk
            mark = jnp.sum(jnp.where(own_lane, spread, 0.0), axis=1, keepdims=True)
            marks = ((lanes.astype(F32) == mark) & (lanes > 0)).astype(BF16)
            values = [flat(rcv1[i, here, t]) for t in range(3)]
            by_head(i, c, jnp.concatenate(values + [marks], axis=1), (0, 1, 2, 4))
        for h in range(i * hb, (i + 1) * hb):
            marks = cell(4, h)
            same = dot(marks, marks, NT) > 0.5
            scores = jnp.where(same, dot(cell(0, h), cell(1, h), NT) * scale, -1e30)
            weights = jnp.exp(scores - jnp.max(scores, axis=1, keepdims=True))
            prob = weights / jnp.sum(weights, axis=1, keepdims=True)
            probs[h] = prob
            keep(0, h, dot(prob.astype(BF16), cell(2, h)))
        for c in range(chunks):
            snda[i, c * peers : (c + 1) * peers] = tiles(by_peer(i, c, (0,)))
        send_rows(snda, rcva, i, 4)

    def backward(i):
        wait_rows(rcvg, i, 2)
        for c in range(chunks):
            by_head(i, c, flat(rcvg[i, c * peers : (c + 1) * peers]), (3,))
        for h in range(i * hb, (i + 1) * hb):
            grads = cell(3, h)
            prob = probs[h]
            attended = outs[0, h].reshape(recv_rows, dh)
            delta = jnp.sum(grads.astype(F32) * attended.astype(F32), axis=1, keepdims=True)
            grad_probs = dot(grads, cell(2, h), NT)
            grad_scores = (prob * (grad_probs - delta)).astype(BF16)
            keep(1, h, dot(grad_scores, cell(1, h)) * scale)
            keep(2, h, dot(grad_scores, cell(0, h), TN) * scale)
            keep(3, h, dot(prob.astype(BF16), grads, TN))
        for c in range(chunks):
            back = by_peer(i, c, (1, 2, 3))
            for t in range(3):
                sndb[i, c * peers : (c + 1) * peers, t] = tiles(back[:, t * dh : (t + 1) * dh])
        send_rows(sndb, rcvb, i, 6)

    weight_core(0)
    wait_recv(mrcv.at[pl.ds(0, ns - 1)], 15)
    forward(0)
    wait_recv(gout.at[pl.ds(0, nt - 1)], 14)
    grad_rows(0)
    weight_core(1)
    forward(1)
    grad_rows(1)
    backward(0)
    attended = []
    for i in range(2):
        wait_rows(rcva, i, 4)
        arrived = flat(rcva[i])
        attended.append(
            jnp.concatenate(
                [dot(unpack[h], arrived).astype(BF16) for h in range(i * hb, (i + 1) * hb)],
                axis=1,
            )
        )

    def project(y, carry):
        rsnd[:, y] = (
            (
                dot(attended[0], wt[0, y].reshape(columns, half), NT)
                + dot(attended[1], wt[1, y].reshape(columns, half), NT)
            )
            .astype(BF16)
            .reshape(nt, tok // nt, columns)
        )

        def scatter(j, inner):
            target = lax.rem(mt + j, nt)
            remote(rsnd.at[target, y], rrcv.at[mt, y], 16, {"tensor": target}).start()
            return inner

        lax.fori_loop(1, nt, scatter, 0)
        rrcv[mt, y] = rsnd[mt, y]
        return carry

    lax.fori_loop(0, ny, project, 0)

    backward(1)

    def deliver(i):
        wait_rows(rcvb, i, 6)
        arrived = jnp.concatenate([flat(rcvb[i, :, t]) for t in range(3)], axis=1)
        for h in range(i * hb, (i + 1) * hb):
            back = dot(unpack[h], arrived).astype(BF16)
            for t, ref in enumerate((dq_ref, dk_ref, dv_ref)):
                ref[:, h * dh : (h + 1) * dh] = back[:, t * dh : (t + 1) * dh]

    deliver(0)
    wait_recv(rrcv.at[pl.ds(0, nt - 1)], 16)
    for y in range(ny):
        total = rrcv[0, y].astype(F32)
        for t in range(1, nt):
            total = total + rrcv[t, y].astype(F32)
        mixed_ref[:, y * columns : (y + 1) * columns] = total.astype(BF16)
    deliver(1)

    for i in range(2):
        wait_send(wt.at[i, pl.ds(0, ny - 1), 0, 0], 8 + i)
        wait_send(wt.at[i, :, pl.ds(0, nx - 1), 0], 10 + i)
        wait_send(wt.at[i, :, :, 0], 12 + i)
    wait_send(gout.at[pl.ds(0, nt - 1)], 14)
    wait_send(msnd.at[pl.ds(0, ns - 1)], 15)
    wait_send(rsnd.at[pl.ds(0, nt - 1)], 16)
    for i in range(2):
        for n, ref in enumerate((snd1, sndg, snda, sndb)):
            wait_send(ref.at[i, pl.ds(0, ns - 1)], 2 * n + i)


def solution(mesh, grid=(8, 4)):
    ny, nx = grid
    ns, nt = mesh.shape["seq"], mesh.shape["tensor"]

    def shards(query_rows, key_rows, value_rows, cluster_id, slot_index, out_weight, grad_out):
        tok = query_rows.shape[0]
        heads = cluster_id.shape[0]
        dh = query_rows.shape[1] // heads
        hb = heads // 2
        blk = hb * SLOTS
        peers = min(32, ns)
        chunks = ns // peers
        rows = peers * blk
        part = peers * SLOTS
        columns = nx * 2 * 32
        vmem = pl.BlockSpec(memory_space=pltpu.VMEM)
        one = pltpu.VMEM((2, ns, blk, dh), BF16)
        three = pltpu.VMEM((2, ns, 3, blk, dh), BF16)
        wide = jax.ShapeDtypeStruct(query_rows.shape, BF16)
        return pl.pallas_call(
            functools.partial(kernel, (ny, nx, nt, heads, tok, dh)),
            out_shape=(jax.ShapeDtypeStruct(grad_out.shape, BF16), wide, wide, wide),
            in_specs=[pl.BlockSpec(memory_space=pltpu.HBM)] * 6,
            out_specs=(vmem,) * 4,
            scratch_shapes=[
                pltpu.VMEM(cluster_id.shape, jnp.int32),
                pltpu.VMEM(out_weight.shape, BF16),
                pltpu.VMEM((2, hb * tok, 3 * dh), BF16),
                pltpu.VMEM((2, chunks, rows, hb * tok), BF16),
                pltpu.VMEM((heads, tok, ns * blk), BF16),
                pltpu.VMEM((ns, 1, 128), F32),
                pltpu.VMEM((ns, 1, 128), F32),
                three,
                three,
                one,
                one,
                one,
                one,
                three,
                three,
                pltpu.VMEM((2, hb * tok, dh), BF16),
                pltpu.VMEM((2, ny, nx, 2, 32, heads * dh // 2), BF16),
                pltpu.VMEM((nt,) + grad_out.shape, BF16),
                pltpu.VMEM((nt, ny, tok // nt, columns), BF16),
                pltpu.VMEM((nt, ny, tok // nt, columns), BF16),
                pltpu.VMEM((5, heads, chunks, part, dh), BF16),
                pltpu.VMEM((heads, ns * SLOTS, ns * SLOTS), F32),
                pltpu.VMEM((4, heads, chunks, part, dh), BF16),
                pltpu.SemaphoreType.DMA((17,)),
                pltpu.SemaphoreType.DMA((17,)),
                pltpu.SemaphoreType.DMA((3 + 3 * heads,)),
            ],
            compiler_params=pltpu.CompilerParams(
                collective_id=0, has_side_effects=True, vmem_limit_bytes=48 * 1024 * 1024
            ),
        )(query_rows, key_rows, value_rows, cluster_id, out_weight, grad_out)

    return jax.shard_map(
        shards,
        mesh=mesh,
        in_specs=(
            P("seq", "tensor"),
            P("seq", "tensor"),
            P("seq", "tensor"),
            P("tensor", "seq"),
            P("tensor", "seq"),
            P("tensor", "seq"),
            P(("seq", "tensor"), None),
        ),
        out_specs=(
            P(("seq", "tensor"), None),
            P("seq", "tensor"),
            P("seq", "tensor"),
            P("seq", "tensor"),
        ),
        check_vma=False,
    )
```
